128 devices in a mesh: pipe: 4 (over z), seq: 16 (over y, x), cfg: 2 (over core).
Axes of the slice: x: 4, y: 4, z: 4, core: 2. Of those that a mesh axis runs over, the one named last changes fastest.
Arguments:
- hidden: bfloat16 [2, 4, 2048, 5120], P('cfg', 'pipe', 'seq'), may hold values from -6 to 6
- qkv_weight: bfloat16 [4, 5120, 3, 4096], P('pipe', None, None, 'seq'), may hold values from -1 to 1
- out_weight: bfloat16 [4, 4096, 5120], P('pipe', 'seq'), may hold values from -0.09375 to 0.09375
- qk_gain: float32 [4, 2, 4096], P('pipe', None, 'seq'), may hold values from 0 to 8
- stale_kv: bfloat16 [2, 4, 2, 4096, 4096], P('cfg', 'pipe', None, None, 'seq'), may hold values from -6 to 6
- modulation: float32 [4, 50, 3, 5120], P('pipe'), may hold values from -3 to 3
- head_mod: float32 [50, 2, 5120], replicated, may hold values from -3 to 3
- head_weight: bfloat16 [5120, 64], replicated, may hold values from -0.078125 to 0.078125
- patch_index: int32 [1], replicated, may hold values from 0 to 1
- timestep: int32 [1], replicated, may hold values from 0 to 49
Outputs:
- forwarded: bfloat16 [2, 4, 2048, 5120], P('cfg', 'pipe', 'seq')
- fresh_kv: bfloat16 [2, 4, 2, 2048, 4096], P('cfg', 'pipe', None, None, 'seq')
- guided: float32 [4, 2048, 64], P('pipe', 'seq', 'cfg')
The draws below stay inside these ranges and needn't reach their ends.
All inputs are finite; a program needn't handle non-finite values.
Results may differ from the reference program's by a relative error of at most 0.01.
Values may be sent and summed in bfloat16 or wider, within the bound.
No kernel may reach another device: no remote copies, remote signals or barrier semaphores. Data moves between devices by JAX's collectives and lax.ppermute only.
A program may use at most 128 MiB of HBM per device.

```python
import math
import jax
import jax.numpy as jnp
from jax import lax

D = 5120
HEADS = 32
HEAD = 128
OUT_CH = 64
STEPS = 50
NPATCH = 2
PT = 2048
HD = 4096
SEQLEN = 4096
N_PIPE = 4
N_SEQ = 16


def chosen_heads(key):
    return jax.random.randint(jax.random.fold_in(key, 7), (N_PIPE,), 0, HEADS)


def chosen_columns(key):
    heads = chosen_heads(key)
    column_head = jnp.arange(HD, dtype=jnp.int32) // HEAD
    return (column_head[None, :] == heads[:, None]).astype(jnp.float32)


def draw_qkv_weight(key, part):
    base = jnp.clip(jax.random.normal(jax.random.fold_in(key, 11), (N_PIPE, D, 3, HD), jnp.float32), -6.0, 6.0)
    marked = chosen_columns(key)[:, None, :]
    query_cols = base[:, :, 0, :]
    tied = (query_cols + 0.25 * base[:, :, 1, :]) * (1.0 / math.sqrt(1.0625))
    key_cols = marked * tied + (1.0 - marked) * base[:, :, 1, :]
    stacked = jnp.stack([query_cols, key_cols, base[:, :, 2, :]], axis=2)
    return (stacked * D ** (-0.5)).astype(jnp.bfloat16)


def draw_qk_gain(key, part):
    first = jax.random.fold_in(key, 13)
    second = jax.random.fold_in(key, 14)
    third = jax.random.fold_in(key, 15)
    gains = 1.0 + 0.15 * jnp.clip(jax.random.normal(first, (N_PIPE, 2, HD), jnp.float32), -5.0, 5.0)
    level = jnp.exp(jax.random.uniform(second, (N_PIPE, 1, 1), jnp.float32, math.log(4.0), math.log(6.0)))
    ripple = 1.0 + 0.1 * jnp.clip(jax.random.normal(third, (N_PIPE, 2, HD), jnp.float32), -3.0, 3.0)
    marked = chosen_columns(key)[:, None, :]
    return marked * level * ripple + (1.0 - marked) * gains


def draw_hidden(key, part):
    first = jax.random.fold_in(key, 17)
    shape = (2, N_PIPE, PT, D)
    return jnp.clip(jax.random.normal(first, shape, jnp.float32), -6.0, 6.0).astype(jnp.bfloat16)


def level_of(key, dims, cuts, smallest, largest):
    level, own = 1.0, jax.random.fold_in(key, 6)
    for axis_at, parts in cuts:
        heights = jnp.exp(jax.random.uniform(jax.random.fold_in(own, axis_at), (parts,), jnp.float32, smallest / len(cuts), largest / len(cuts)))
        level = level * jnp.repeat(heights, dims[axis_at] // parts).reshape([-1 if axis == axis_at else 1 for axis in range(len(dims))])
    return level


def scatter_about(own_key, dims, width, most, pieces=(), held_as=jnp.bfloat16):
    drawn = jax.random.normal(own_key, dims, jnp.float32) * width
    if len(pieces) > 0:
        drawn = level_of(own_key, dims, pieces, -0.22, 0.18) * drawn
    return jnp.clip(drawn, min=-most, max=most).astype(held_as)


def setup_inputs(seed: int = 0) -> dict:
    splits = jax.random.split(jax.random.key(seed), 11)
    hidden = draw_hidden(jax.random.fold_in(splits[10], 71), 0)
    qkv_weight = draw_qkv_weight(jax.random.fold_in(splits[10], 71), 0)
    out_weight = scatter_about(splits[2], (N_PIPE, HD, D), HD ** -0.5, 0.09375, ((0, 4), (1, 16)))
    qk_gain = draw_qk_gain(jax.random.fold_in(splits[10], 71), 0)
    stale_kv = scatter_about(splits[4], (2, N_PIPE, 2, SEQLEN, HD), 1.0, 6.0, ((0, 2), (1, 4), (4, 16)))
    modulation = scatter_about(splits[5], (N_PIPE, STEPS, 3, D), 0.5, 3.0, ((0, 4),), jnp.float32)
    head_mod = scatter_about(splits[6], (STEPS, 2, D), 0.5, 3.0, (), jnp.float32)
    head_weight = scatter_about(splits[7], (D, OUT_CH), D ** -0.5, 0.078125)
    patch_index = jax.random.randint(splits[8], (1,), 0, NPATCH).astype(jnp.int32)
    timestep = jax.random.randint(splits[9], (1,), 0, STEPS).astype(jnp.int32)
    return {"hidden": hidden, "qkv_weight": qkv_weight, "out_weight": out_weight, "qk_gain": qk_gain, "stale_kv": stale_kv, "modulation": modulation, "head_mod": head_mod, "head_weight": head_weight, "patch_index": patch_index, "timestep": timestep}


epsilon = 1e-06
guidance = 5.0

def modulate(inputs, shift_row, scale_row):
    values = inputs.astype(jnp.float32)
    center = lax.optimization_barrier(jnp.mean(values, axis=-1, keepdims=True))
    spread = lax.optimization_barrier(jnp.mean(jnp.square(values - center), axis=-1, keepdims=True))
    return (values - center) * lax.rsqrt(spread + epsilon) * (1.0 + scale_row) + shift_row

def attend_head(operands):
    queries, key_rows, value_rows = operands
    scores = jnp.dot(queries, key_rows.T, preferred_element_type=jnp.float32) * HEAD ** (-0.5)
    top = lax.optimization_barrier(jnp.max(scores, axis=-1, keepdims=True))
    expo = jnp.exp(scores - top)
    weights = (expo / lax.optimization_barrier(jnp.sum(expo, axis=-1, keepdims=True))).astype(jnp.bfloat16)
    return jnp.dot(weights, value_rows, preferred_element_type=jnp.float32).astype(jnp.bfloat16)

def add_group(carry, operands):
    attn_part, weight_part = operands
    term = jnp.dot(attn_part, weight_part, preferred_element_type=jnp.float32).astype(jnp.bfloat16)
    term = lax.optimization_barrier(term)
    return (carry + term.astype(jnp.float32), None)

def run_section(inputs, qkv_rows, out_rows, qk_gains, stale_pair, mod_rows, patch_slot):
    tokens = inputs.shape[0]
    normed = modulate(inputs, mod_rows[0], mod_rows[1]).astype(jnp.bfloat16)
    projections = jnp.dot(normed, qkv_rows.reshape(D, 3 * HD), preferred_element_type=jnp.float32)
    queries = projections[:, :HD]
    key_cols = projections[:, HD:2 * HD]
    value_cols = projections[:, 2 * HD:]
    query_scale = lax.rsqrt(lax.optimization_barrier(jnp.mean(jnp.square(queries), axis=-1, keepdims=True)) + epsilon)
    key_scale = lax.rsqrt(lax.optimization_barrier(jnp.mean(jnp.square(key_cols), axis=-1, keepdims=True)) + epsilon)
    query_normed = (queries * query_scale * qk_gains[0]).astype(jnp.bfloat16)
    key_normed = (key_cols * key_scale * qk_gains[1]).astype(jnp.bfloat16)
    value_normed = value_cols.astype(jnp.bfloat16)
    first_row = (patch_slot * tokens).astype(jnp.int32)
    key_set = lax.dynamic_update_slice(stale_pair[0], key_normed, (first_row, jnp.int32(0)))
    value_set = lax.dynamic_update_slice(stale_pair[1], value_normed, (first_row, jnp.int32(0)))
    query_heads = query_normed.reshape(tokens, HEADS, HEAD).transpose(1, 0, 2)
    key_heads = key_set.reshape(SEQLEN, HEADS, HEAD).transpose(1, 0, 2)
    value_heads = value_set.reshape(SEQLEN, HEADS, HEAD).transpose(1, 0, 2)
    attended = lax.map(attend_head, (query_heads, key_heads, value_heads))
    attended = attended.transpose(1, 0, 2).reshape(tokens, HD)
    group_width = HD // N_SEQ
    attn_groups = attended.reshape(tokens, N_SEQ, group_width).transpose(1, 0, 2)
    weight_groups = out_rows.reshape(N_SEQ, group_width, D)
    projected, _ = lax.scan(add_group, jnp.zeros((tokens, D), jnp.float32), (attn_groups, weight_groups))
    result = (inputs.astype(jnp.float32) + mod_rows[2] * projected).astype(jnp.bfloat16)
    return (result, jnp.stack([key_normed, value_normed]))

def reference(hidden, qkv_weight, out_weight, qk_gain, stale_kv, modulation, head_mod, head_weight, patch_index, timestep):
    step_row = timestep[0]
    head_rows = lax.dynamic_index_in_dim(head_mod, step_row, 0, keepdims=False)
    results = []
    fresh_all = []
    readouts = []
    for branch in range(2):
        branch_results = []
        branch_fresh = []
        branch_reads = []
        for section_index in range(N_PIPE):
            mod_rows = lax.dynamic_index_in_dim(modulation[section_index], step_row, 0, keepdims=False)
            patch_slot = jnp.mod(patch_index[0] - section_index, NPATCH)
            result, fresh_pair = run_section(hidden[branch, section_index], qkv_weight[section_index], out_weight[section_index], qk_gain[section_index], stale_kv[branch, section_index], mod_rows, patch_slot)
            normed_out = modulate(result, head_rows[0], head_rows[1]).astype(jnp.bfloat16)
            branch_reads.append(jnp.dot(normed_out, head_weight, preferred_element_type=jnp.float32))
            branch_results.append(result)
            branch_fresh.append(fresh_pair)
        results.append(branch_results)
        fresh_all.append(jnp.stack(branch_fresh))
        readouts.append(branch_reads)
    forwarded = jnp.stack([jnp.stack([results[branch][(section_index - 1) % N_PIPE] for section_index in range(N_PIPE)]) for branch in range(2)])
    fresh_kv = jnp.stack(fresh_all)
    guided = jnp.stack([readouts[1][section_index] + guidance * (readouts[0][section_index] - readouts[1][section_index]) for section_index in range(N_PIPE)])
    return (forwarded, fresh_kv, guided)
```

```python
import functools
import math

import jax
import jax.numpy as jnp
from jax import lax
from jax.experimental import pallas as pl
from jax.experimental.pallas import tpu as pltpu
from jax.sharding import Mesh, PartitionSpec as P

HEAD = 128
NPATCH = 2
epsilon = 1e-06
guidance = 5.0
SCORE = math.log2(math.e) * HEAD**-0.5
LAST = (((1,), (1,)), ((), ()))


def passed_along(block, axis, distance):
    devices = range(lax.axis_size(axis))
    route = [((i - distance) % len(devices), i) for i in devices]
    return lax.ppermute(block, axis, route)


def partner_2(shard, axis, stride):
    return lax.ppermute(shard, axis, [(i, i ^ stride) for i in range(lax.axis_size(axis))])


def butterfly_sum(value):
    for axis in ("x", "y"):
        for stride in (1, 2):
            value = value + partner_2(value, axis, stride)
    return value


def modulate(inputs, shift_row, scale_row):
    values = inputs.astype(jnp.float32)
    center = jnp.mean(values, axis=-1, keepdims=True)
    spread = jnp.mean(jnp.square(values - center), axis=-1, keepdims=True)
    return (values - center) * lax.rsqrt(spread + epsilon) * (1.0 + scale_row) + shift_row


def norm_body(step_ref, x_ref, mod_ref, out_ref):
    out_ref[...] = modulate(x_ref[...], mod_ref[0, 0:1, :], mod_ref[0, 1:2, :]).astype(
        jnp.bfloat16
    )


def norm_rows(timestep, tokens, table):
    rows, width = tokens.shape
    part = rows // 4
    return pl.pallas_call(
        norm_body,
        grid_spec=pltpu.PrefetchScalarGridSpec(
            num_scalar_prefetch=1,
            grid=(4,),
            in_specs=[
                pl.BlockSpec((part, width), lambda i, t: (i, 0)),
                pl.BlockSpec((1,) + table.shape[1:], lambda i, t: (t[0], 0, 0)),
            ],
            out_specs=pl.BlockSpec((part, width), lambda i, t: (i, 0)),
        ),
        out_shape=jax.ShapeDtypeStruct((rows, width), jnp.bfloat16),
    )(timestep, tokens, table)


def attend_body(slot_ref, q_ref, kf, vf, ks, vs, out_ref):
    queries = q_ref[...]
    top = total = mixed = None
    for keys, values in ((kf, vf), (ks, vs)):
        scores = lax.dot_general(queries, keys[0], LAST, preferred_element_type=jnp.float32)
        high = jnp.max(scores, axis=-1, keepdims=True) * SCORE
        new_top = high if top is None else jnp.maximum(top, high)
        expo = jnp.exp2(scores * SCORE - new_top)
        part = jnp.sum(expo, axis=-1, keepdims=True)
        term = jnp.dot(expo.astype(jnp.bfloat16), values[0], preferred_element_type=jnp.float32)
        if top is None:
            total, mixed = part, term
        else:
            decay = jnp.exp2(top - new_top)
            total, mixed = total * decay + part, mixed * decay + term
        top = new_top
    out_ref[...] = (mixed / total).astype(jnp.bfloat16)


def attend(other_slot, queries, fresh, stale, block):
    rows, width = queries.shape
    keys = fresh.shape[1]
    return pl.pallas_call(
        attend_body,
        grid_spec=pltpu.PrefetchScalarGridSpec(
            num_scalar_prefetch=1,
            grid=(width // HEAD, rows // block),
            in_specs=[
                pl.BlockSpec((block, HEAD), lambda h, i, s: (i, h)),
                pl.BlockSpec((1, keys, HEAD), lambda h, i, s: (0, 0, h)),
                pl.BlockSpec((1, keys, HEAD), lambda h, i, s: (1, 0, h)),
                pl.BlockSpec((1, keys, HEAD), lambda h, i, s: (0, s[0], h)),
                pl.BlockSpec((1, keys, HEAD), lambda h, i, s: (1, s[0], h)),
            ],
            out_specs=pl.BlockSpec((block, HEAD), lambda h, i, s: (i, h)),
        ),
        out_shape=jax.ShapeDtypeStruct((rows, width), jnp.bfloat16),
        compiler_params=pltpu.CompilerParams(vmem_limit_bytes=56 * 2**20),
        cost_estimate=pl.CostEstimate(
            flops=8 * rows * keys * width,
            bytes_accessed=8 * keys * width,
            transcendentals=4 * rows * keys,
        ),
    )(other_slot, queries, fresh, fresh, stale, stale)


def per_device(
    hidden,
    qkv_weight,
    out_weight,
    qk_gain,
    stale_kv,
    modulation,
    head_mod,
    head_weight,
    patch_index,
    timestep,
):
    tokens_in = hidden[0, 0]
    step_row = timestep[0]
    in_weight = qkv_weight[0]
    model_width = in_weight.shape[0]
    local_width = in_weight.shape[2]
    in_weight = in_weight.reshape(model_width, 3 * local_width)
    normed = norm_rows(timestep, tokens_in, modulation[0])
    gathered = lax.all_gather(normed, ("y", "x"), axis=0, tiled=True)
    projections = jnp.dot(gathered, in_weight, preferred_element_type=jnp.float32)
    queries = projections[:, :local_width]
    key_cols = projections[:, local_width : 2 * local_width]
    value_cols = projections[:, 2 * local_width :]
    square_sums = butterfly_sum(
        jnp.stack([jnp.sum(jnp.square(queries), -1), jnp.sum(jnp.square(key_cols), -1)])
    )
    full_width = local_width * lax.axis_size(("y", "x"))
    scales = lax.rsqrt(square_sums / full_width + epsilon)[:, :, None]
    query_normed = (queries * scales[0] * qk_gain[0, 0]).astype(jnp.bfloat16)
    key_normed = (key_cols * scales[1] * qk_gain[0, 1]).astype(jnp.bfloat16)
    fresh_pair = jnp.stack([key_normed, value_cols.astype(jnp.bfloat16)])
    patch_slot = jnp.mod(patch_index - lax.axis_index("pipe"), NPATCH)
    attended = attend(1 - patch_slot, query_normed, fresh_pair, stale_kv[0, 0], 512)
    projected = lax.psum_scatter(
        jnp.dot(attended, out_weight[0], preferred_element_type=jnp.float32).astype(jnp.bfloat16),
        ("y", "x"),
        scatter_dimension=0,
        tiled=True,
    ).astype(jnp.float32)
    gate = lax.dynamic_slice(modulation[0], (step_row, 2, 0), (1, 1, model_width))[0]
    block_out = (tokens_in.astype(jnp.float32) + gate * projected).astype(jnp.bfloat16)
    forwarded = passed_along(block_out, "pipe", 1)
    head_rows = lax.dynamic_index_in_dim(head_mod, step_row, 0, keepdims=False)
    normed_out = modulate(block_out, head_rows[0], head_rows[1]).astype(jnp.bfloat16)
    readout = jnp.dot(normed_out, head_weight, preferred_element_type=jnp.float32)
    branch_index = lax.axis_index("cfg")
    half_width = readout.shape[1] // 2
    partner = partner_2(readout.astype(jnp.bfloat16), "cfg", 1).astype(readout.dtype)
    conditional = jnp.where(branch_index == 0, readout, partner)
    unconditional = jnp.where(branch_index == 0, partner, readout)
    combined = unconditional + guidance * (conditional - unconditional)
    guided = lax.dynamic_slice_in_dim(combined, branch_index * half_width, half_width, 1)
    return (forwarded[None, None], fresh_pair[None, None], guided[None])


def solution(mesh):
    sizes = (mesh.shape["pipe"], 4, mesh.shape["seq"] // 4, mesh.shape["cfg"])
    grid = Mesh(mesh.devices.reshape(sizes), ("pipe", "y", "x", "cfg"))
    seq = ("y", "x")
    return jax.shard_map(
        per_device,
        mesh=grid,
        in_specs=(
            P("cfg", "pipe", seq, None),
            P("pipe", None, None, seq),
            P("pipe", seq, None),
            P("pipe", None, seq),
            P("cfg", "pipe", None, None, seq),
            P("pipe", None, None, None),
            P(),
            P(),
            P(),
            P(),
        ),
        out_specs=(
            P("cfg", "pipe", seq, None),
            P("cfg", "pipe", None, None, seq),
            P("pipe", seq, "cfg"),
        ),
        check_vma=False,
    )
```

```python
import functools
import math

import jax
import jax.numpy as jnp
from jax import lax
from jax.experimental import pallas as pl
from jax.experimental.pallas import tpu as pltpu
from jax.sharding import Mesh, PartitionSpec as P

HEAD = 128
NPATCH = 2
epsilon = 1e-06
guidance = 5.0
SCORE = math.log2(math.e) * HEAD**-0.5
LAST = (((1,), (1,)), ((), ()))


def passed_along(block, axis, distance):
    devices = range(lax.axis_size(axis))
    route = [((i - distance) % len(devices), i) for i in devices]
    return lax.ppermute(block, axis, route)


def partner_2(shard, axis, stride):
    return lax.ppermute(shard, axis, [(i, i ^ stride) for i in range(lax.axis_size(axis))])


def butterfly_sum(value):
    for axis in ("x", "y"):
        for stride in (1, 2):
            value = value + partner_2(value, axis, stride)
    return value


def modulate(inputs, shift_row, scale_row):
    values = inputs.astype(jnp.float32)
    center = jnp.mean(values, axis=-1, keepdims=True)
    spread = jnp.mean(jnp.square(values - center), axis=-1, keepdims=True)
    return (values - center) * lax.rsqrt(spread + epsilon) * (1.0 + scale_row) + shift_row


def norm_body(x_ref, mod_ref, out_ref):
    out_ref[...] = modulate(x_ref[...], mod_ref[0:1, :], mod_ref[1:2, :]).astype(jnp.bfloat16)


def norm_rows(tokens, table):
    rows, width = tokens.shape
    part = rows // 4
    return pl.pallas_call(
        norm_body,
        grid=(4,),
        in_specs=[
            pl.BlockSpec((part, width), lambda i: (i, 0)),
            pl.BlockSpec(table.shape, lambda i: (0, 0)),
        ],
        out_specs=pl.BlockSpec((part, width), lambda i: (i, 0)),
        out_shape=jax.ShapeDtypeStruct((rows, width), jnp.bfloat16),
    )(tokens, table)


def attend_body(where_ref, q_ref, kf, vf, ks, vs, out_ref):
    queries = q_ref[...].reshape(out_ref.shape)
    top = total = mixed = None
    for keys, values in ((kf, vf), (ks, vs)):
        scores = lax.dot_general(queries, keys[0], LAST, preferred_element_type=jnp.float32)
        high = jnp.max(scores, axis=-1, keepdims=True) * SCORE
        new_top = high if top is None else jnp.maximum(top, high)
        expo = jnp.exp2(scores * SCORE - new_top)
        part = jnp.sum(expo, axis=-1, keepdims=True)
        term = jnp.dot(expo.astype(jnp.bfloat16), values[0], preferred_element_type=jnp.float32)
        if top is None:
            total, mixed = part, term
        else:
            decay = jnp.exp2(top - new_top)
            total, mixed = total * decay + part, mixed * decay + term
        top = new_top
    out_ref[...] = (mixed / total).astype(jnp.bfloat16)


def attend(where, queries, fresh, stale):
    groups, columns, width = queries.shape
    part = columns // lax.axis_size("x")
    rows = groups * part
    keys = fresh.shape[1]
    return pl.pallas_call(
        attend_body,
        grid_spec=pltpu.PrefetchScalarGridSpec(
            num_scalar_prefetch=1,
            grid=(width // HEAD,),
            in_specs=[
                pl.BlockSpec((groups, part, HEAD), lambda h, w: (0, w[1], h)),
                pl.BlockSpec((1, keys, HEAD), lambda h, w: (0, 0, h)),
                pl.BlockSpec((1, keys, HEAD), lambda h, w: (1, 0, h)),
                pl.BlockSpec((1, keys, HEAD), lambda h, w: (0, w[0], h)),
                pl.BlockSpec((1, keys, HEAD), lambda h, w: (1, w[0], h)),
            ],
            out_specs=pl.BlockSpec((rows, HEAD), lambda h, w: (0, h)),
        ),
        out_shape=jax.ShapeDtypeStruct((rows, width), jnp.bfloat16),
        compiler_params=pltpu.CompilerParams(vmem_limit_bytes=56 * 2**20),
        cost_estimate=pl.CostEstimate(
            flops=8 * rows * keys * width,
            bytes_accessed=8 * keys * width,
            transcendentals=4 * rows * keys,
        ),
    )(where, queries, fresh, fresh, stale, stale)


def project_body(where_ref, *refs):
    count = (len(refs) - 1) // 4
    left = jnp.concatenate([ref[...] for ref in refs[: 2 * count]], axis=1)
    right = jnp.concatenate([ref[0] for ref in refs[2 * count : -1]], axis=0)
    refs[-1][...] = jnp.dot(left, right, preferred_element_type=jnp.float32).astype(jnp.bfloat16)


def project(where, shares, own, other, block):
    count = len(shares)
    rows = shares[0].shape[0] // lax.axis_size("y")
    half = own.shape[1]
    width = own.shape[2]
    left_specs = []
    right_specs = []
    for j in range(count):
        left_specs += [
            pl.BlockSpec((rows, half), lambda i, w: (w[0], w[1])),
            pl.BlockSpec((rows, half), lambda i, w: (w[0], 1 - w[1])),
        ]
        right_specs += [
            pl.BlockSpec((1, half, block), lambda i, w, j=j: (w[2 + j], 0, i)),
            pl.BlockSpec((1, half, block), lambda i, w, j=j: (w[2 + j], 0, i)),
        ]
    lefts = [share for share in shares for _ in range(2)]
    return pl.pallas_call(
        project_body,
        grid_spec=pltpu.PrefetchScalarGridSpec(
            num_scalar_prefetch=1,
            grid=(width // block,),
            in_specs=left_specs + right_specs,
            out_specs=pl.BlockSpec((rows, block), lambda i, w: (0, i)),
        ),
        out_shape=jax.ShapeDtypeStruct((rows, width), jnp.bfloat16),
        compiler_params=pltpu.CompilerParams(vmem_limit_bytes=56 * 2**20),
        cost_estimate=pl.CostEstimate(
            flops=4 * rows * count * half * width,
            bytes_accessed=4 * count * half * width,
            transcendentals=0,
        ),
    )(where, *lefts, *([own, other] * count))


def add_rows(one, two):
    return (one.astype(jnp.float32) + two.astype(jnp.float32)).astype(jnp.bfloat16)


def per_device(
    hidden,
    qkv_weight,
    out_weight,
    qk_gain,
    stale_kv,
    modulation,
    head_mod,
    head_weight,
    patch_index,
    timestep,
):
    tokens_in = hidden[0, 0]
    step_row = timestep[0]
    in_weight = qkv_weight[0]
    model_width = in_weight.shape[0]
    local_width = in_weight.shape[2]
    in_weight = in_weight.reshape(model_width, 3 * local_width)
    mod_rows = lax.dynamic_index_in_dim(modulation[0], step_row, 0, keepdims=False)
    normed = norm_rows(tokens_in, mod_rows)
    gathered = lax.all_gather(normed, ("y", "x"), axis=0, tiled=True)
    x_index, y_index, core = (lax.axis_index(name) for name in ("x", "y", "cfg"))
    half = out_weight.shape[1] // 2
    mine = lax.dynamic_slice_in_dim(out_weight[0], core * half, half, 0)
    gathered, mine = lax.optimization_barrier((gathered, mine))
    own_weights = lax.all_gather(mine, "x", axis=0)
    other_weights = partner_2(own_weights, "cfg", 1)
    projections = jnp.dot(gathered, in_weight, preferred_element_type=jnp.float32)
    queries = projections[:, :local_width]
    key_cols = projections[:, local_width : 2 * local_width]
    value_cols = projections[:, 2 * local_width :]
    square_sums = butterfly_sum(
        jnp.stack([jnp.sum(jnp.square(queries), -1), jnp.sum(jnp.square(key_cols), -1)])
    )
    full_width = local_width * lax.axis_size(("y", "x"))
    scales = lax.rsqrt(square_sums / full_width + epsilon)[:, :, None]
    query_normed = (queries * scales[0] * qk_gain[0, 0]).astype(jnp.bfloat16)
    key_normed = (key_cols * scales[1] * qk_gain[0, 1]).astype(jnp.bfloat16)
    fresh_pair = jnp.stack([key_normed, value_cols.astype(jnp.bfloat16)])
    patch_slot = jnp.mod(patch_index - lax.axis_index("pipe"), NPATCH)
    columns, lines = lax.axis_size("x"), lax.axis_size("y")
    query_groups = query_normed.reshape(lines, -1, local_width)
    shares = {}
    for j in (2, 1, 3, 0):
        where = jnp.concatenate([1 - patch_slot, ((x_index + j) % columns)[None]])
        block = attend(where, query_groups, fresh_pair, stale_kv[0, 0])
        shares[j] = passed_along(block, "x", j) if j else block
    sources = [(x_index - j) % columns for j in range(columns)]

    def rows_for(k):
        where = jnp.stack([(y_index + k) % lines, core] + sources).astype(jnp.int32)
        return project(where, [shares[j] for j in range(columns)], own_weights, other_weights, 1024)

    cut = tokens_in.shape[0] // 2
    across = rows_for(2)
    from_below = passed_along(across[:cut], "y", 1)
    from_above = passed_along(across[cut:], "y", 3)
    up = rows_for(1)
    low_up = passed_along(up[cut:], "y", 1)
    down = rows_for(3)
    high_down = passed_along(down[:cut], "y", 3)
    high_up = passed_along(add_rows(up[:cut], from_below), "y", 1)
    low_down = passed_along(add_rows(down[cut:], from_above), "y", 3)
    projected = rows_for(0).astype(jnp.float32) + jnp.concatenate(
        [
            high_up.astype(jnp.float32) + high_down.astype(jnp.float32),
            low_up.astype(jnp.float32) + low_down.astype(jnp.float32),
        ]
    )
    gate = mod_rows[2:3]
    block_out = (tokens_in.astype(jnp.float32) + gate * projected).astype(jnp.bfloat16)
    forwarded = passed_along(block_out, "pipe", 1)
    head_rows = lax.dynamic_index_in_dim(head_mod, step_row, 0, keepdims=False)
    normed_out = modulate(block_out, head_rows[0], head_rows[1]).astype(jnp.bfloat16)
    readout = jnp.dot(normed_out, head_weight, preferred_element_type=jnp.float32)
    branch_index = lax.axis_index("cfg")
    half_width = readout.shape[1] // 2
    partner = partner_2(readout.astype(jnp.bfloat16), "cfg", 1).astype(readout.dtype)
    conditional = jnp.where(branch_index == 0, readout, partner)
    unconditional = jnp.where(branch_index == 0, partner, readout)
    combined = unconditional + guidance * (conditional - unconditional)
    guided = lax.dynamic_slice_in_dim(combined, branch_index * half_width, half_width, 1)
    return (forwarded[None, None], fresh_pair[None, None], guided[None])


def solution(mesh):
    sizes = (mesh.shape["pipe"], 4, mesh.shape["seq"] // 4, mesh.shape["cfg"])
    grid = Mesh(mesh.devices.reshape(sizes), ("pipe", "y", "x", "cfg"))
    seq = ("y", "x")
    return jax.shard_map(
        per_device,
        mesh=grid,
        in_specs=(
            P("cfg", "pipe", seq, None),
            P("pipe", None, None, seq),
            P("pipe", seq, None),
            P("pipe", None, seq),
            P("cfg", "pipe", None, None, seq),
            P("pipe", None, None, None),
            P(),
            P(),
            P(),
            P(),
        ),
        out_specs=(
            P("cfg", "pipe", seq, None),
            P("cfg", "pipe", None, None, seq),
            P("pipe", seq, "cfg"),
        ),
        check_vma=False,
    )
```

```python
import functools
import math

import jax
import jax.numpy as jnp
from jax import lax
from jax.experimental import pallas as pl
from jax.experimental.pallas import tpu as pltpu
from jax.sharding import Mesh, PartitionSpec as P

HEAD = 128
NPATCH = 2
epsilon = 1e-06
guidance = 5.0
SCORE = math.log2(math.e) * HEAD**-0.5
LAST = (((1,), (1,)), ((), ()))


def passed_along(block, axis, distance):
    devices = range(lax.axis_size(axis))
    route = [((i - distance) % len(devices), i) for i in devices]
    return lax.ppermute(block, axis, route)


def partner_2(shard, axis, stride):
    return lax.ppermute(shard, axis, [(i, i ^ stride) for i in range(lax.axis_size(axis))])


def butterfly_sum(value):
    for axis in ("x", "y"):
        for stride in (1, 2):
            value = value + partner_2(value, axis, stride)
    return value


def modulate(inputs, shift_row, scale_row):
    values = inputs.astype(jnp.float32)
    center = jnp.mean(values, axis=-1, keepdims=True)
    spread = jnp.mean(jnp.square(values - center), axis=-1, keepdims=True)
    return (values - center) * lax.rsqrt(spread + epsilon) * (1.0 + scale_row) + shift_row


def norm_body(x_ref, mod_ref, out_ref):
    out_ref[...] = modulate(x_ref[...], mod_ref[0:1, :], mod_ref[1:2, :]).astype(jnp.bfloat16)


def norm_rows(tokens, table):
    rows, width = tokens.shape
    part = rows // 4
    return pl.pallas_call(
        norm_body,
        grid=(4,),
        in_specs=[
            pl.BlockSpec((part, width), lambda i: (i, 0)),
            pl.BlockSpec(table.shape, lambda i: (0, 0)),
        ],
        out_specs=pl.BlockSpec((part, width), lambda i: (i, 0)),
        out_shape=jax.ShapeDtypeStruct((rows, width), jnp.bfloat16),
    )(tokens, table)


def attend_body(where_ref, q_ref, kf, vf, ks, vs, out_ref):
    queries = q_ref[...].reshape(out_ref.shape)
    top = total = mixed = None
    for keys, values in ((kf, vf), (ks, vs)):
        scores = lax.dot_general(queries, keys[0], LAST, preferred_element_type=jnp.float32)
        high = jnp.max(scores, axis=-1, keepdims=True) * SCORE
        new_top = high if top is None else jnp.maximum(top, high)
        expo = jnp.exp2(scores * SCORE - new_top)
        part = jnp.sum(expo, axis=-1, keepdims=True)
        term = jnp.dot(expo.astype(jnp.bfloat16), values[0], preferred_element_type=jnp.float32)
        if top is None:
            total, mixed = part, term
        else:
            decay = jnp.exp2(top - new_top)
            total, mixed = total * decay + part, mixed * decay + term
        top = new_top
    out_ref[...] = (mixed / total).astype(jnp.bfloat16)


def attend(where, queries, fresh, stale):
    groups, columns, width = queries.shape
    part = columns // lax.axis_size("x")
    rows = groups * part
    keys = fresh.shape[1]
    return pl.pallas_call(
        attend_body,
        grid_spec=pltpu.PrefetchScalarGridSpec(
            num_scalar_prefetch=1,
            grid=(width // HEAD,),
            in_specs=[
                pl.BlockSpec((groups, part, HEAD), lambda h, w: (0, w[1], h)),
                pl.BlockSpec((1, keys, HEAD), lambda h, w: (0, 0, h)),
                pl.BlockSpec((1, keys, HEAD), lambda h, w: (1, 0, h)),
                pl.BlockSpec((1, keys, HEAD), lambda h, w: (0, w[0], h)),
                pl.BlockSpec((1, keys, HEAD), lambda h, w: (1, w[0], h)),
            ],
            out_specs=pl.BlockSpec((rows, HEAD), lambda h, w: (0, h)),
        ),
        out_shape=jax.ShapeDtypeStruct((rows, width), jnp.bfloat16),
        compiler_params=pltpu.CompilerParams(vmem_limit_bytes=56 * 2**20),
        cost_estimate=pl.CostEstimate(
            flops=8 * rows * keys * width,
            bytes_accessed=8 * keys * width,
            transcendentals=4 * rows * keys,
        ),
    )(where, queries, fresh, fresh, stale, stale)


def project_body(where_ref, *refs, sources, groups):
    lefts, refs = refs[: 2 * sources * groups], refs[2 * sources * groups :]
    rights, outs = refs[: 2 * sources], refs[2 * sources :]
    left = jnp.concatenate(
        [
            jnp.concatenate([ref[...] for ref in lefts[g * 2 * sources : (g + 1) * 2 * sources]], 1)
            for g in range(groups)
        ],
        axis=0,
    )
    right = jnp.concatenate([ref[0] for ref in rights], axis=0)
    terms = jnp.dot(left, right, preferred_element_type=jnp.float32).astype(jnp.bfloat16)
    cut = outs[0].shape[0]
    for n, out in enumerate(outs):
        out[...] = terms[n * cut : (n + 1) * cut]


def project(where, groups, shares, own, other, block):
    count = len(shares)
    rows = shares[0].shape[0] // lax.axis_size("y")
    half = own.shape[1]
    width = own.shape[2]
    left_specs = []
    right_specs = []
    for g in range(groups):
        for _ in range(count):
            left_specs += [
                pl.BlockSpec((rows, half), lambda i, w, g=g: (w[1 + count + g], w[0])),
                pl.BlockSpec((rows, half), lambda i, w, g=g: (w[1 + count + g], 1 - w[0])),
            ]
    for j in range(count):
        right_specs += 2 * [pl.BlockSpec((1, half, block), lambda i, w, j=j: (w[1 + j], 0, i))]
    lefts = [share for share in shares for _ in range(2)] * groups
    return pl.pallas_call(
        functools.partial(project_body, sources=count, groups=groups),
        grid_spec=pltpu.PrefetchScalarGridSpec(
            num_scalar_prefetch=1,
            grid=(width // block,),
            in_specs=left_specs + right_specs,
            out_specs=[pl.BlockSpec((rows // 2, block), lambda i, w: (0, i))] * (2 * groups),
        ),
        out_shape=[jax.ShapeDtypeStruct((rows // 2, width), jnp.bfloat16)] * (2 * groups),
        compiler_params=pltpu.CompilerParams(vmem_limit_bytes=56 * 2**20),
        cost_estimate=pl.CostEstimate(
            flops=4 * groups * rows * count * half * width,
            bytes_accessed=4 * count * half * width,
            transcendentals=0,
        ),
    )(where, *lefts, *([own, other] * count))


def add_rows(one, two):
    return (one.astype(jnp.float32) + two.astype(jnp.float32)).astype(jnp.bfloat16)


def per_device(
    hidden,
    qkv_weight,
    out_weight,
    qk_gain,
    stale_kv,
    modulation,
    head_mod,
    head_weight,
    patch_index,
    timestep,
):
    tokens_in = hidden[0, 0]
    step_row = timestep[0]
    in_weight = qkv_weight[0]
    model_width = in_weight.shape[0]
    local_width = in_weight.shape[2]
    in_weight = in_weight.reshape(model_width, 3 * local_width)
    mod_rows = lax.dynamic_index_in_dim(modulation[0], step_row, 0, keepdims=False)
    normed = norm_rows(tokens_in, mod_rows)
    gathered = lax.all_gather(normed, ("y", "x"), axis=0, tiled=True)
    x_index, y_index, core = (lax.axis_index(name) for name in ("x", "y", "cfg"))
    half = out_weight.shape[1] // 2
    mine = lax.dynamic_slice_in_dim(out_weight[0], core * half, half, 0)
    gathered, mine = lax.optimization_barrier((gathered, mine))
    own_weights = lax.all_gather(mine, "x", axis=0)
    projections = jnp.dot(gathered, in_weight, preferred_element_type=jnp.float32)
    queries = projections[:, :local_width]
    key_cols = projections[:, local_width : 2 * local_width]
    value_cols = projections[:, 2 * local_width :]
    square_sums = butterfly_sum(
        jnp.stack([jnp.sum(jnp.square(queries), -1), jnp.sum(jnp.square(key_cols), -1)])
    )
    full_width = local_width * lax.axis_size(("y", "x"))
    scales = lax.rsqrt(square_sums / full_width + epsilon)[:, :, None]
    query_normed = (queries * scales[0] * qk_gain[0, 0]).astype(jnp.bfloat16)
    key_normed = (key_cols * scales[1] * qk_gain[0, 1]).astype(jnp.bfloat16)
    fresh_pair = jnp.stack([key_normed, value_cols.astype(jnp.bfloat16)])
    patch_slot = jnp.mod(patch_index - lax.axis_index("pipe"), NPATCH)
    columns, lines = lax.axis_size("x"), lax.axis_size("y")
    query_groups = query_normed.reshape(lines, -1, local_width)
    shares = {}
    for j in (2, 1, 3, 0):
        where = jnp.concatenate([1 - patch_slot, ((x_index + j) % columns)[None]])
        block = attend(where, query_groups, fresh_pair, stale_kv[0, 0])
        if j == 2:
            own_weights = lax.optimization_barrier((own_weights, block))[0]
            other_weights = partner_2(own_weights, "cfg", 1)
        shares[j] = passed_along(block, "x", j) if j else block
    sources = [(x_index - j) % columns for j in range(columns)]

    def rows_for(*places):
        where = [core] + sources + [(y_index + k) % lines for k in places]
        return project(
            jnp.stack(where).astype(jnp.int32),
            len(places),
            [shares[j] for j in range(columns)],
            own_weights,
            other_weights,
            1024,
        )

    high_across, low_across = rows_for(2)
    from_below = passed_along(high_across, "y", 1)
    from_above = passed_along(low_across, "y", 3)
    up_high, up_low, down_high, down_low = rows_for(1, 3)
    low_up = passed_along(up_low, "y", 1)
    high_down = passed_along(down_high, "y", 3)
    high_up = passed_along(add_rows(up_high, from_below), "y", 1)
    low_down = passed_along(add_rows(down_low, from_above), "y", 3)
    high, low = (part.astype(jnp.float32) for part in rows_for(0))
    projected = jnp.concatenate(
        [
            high + high_up.astype(jnp.float32) + high_down.astype(jnp.float32),
            low + low_up.astype(jnp.float32) + low_down.astype(jnp.float32),
        ]
    )
    gate = mod_rows[2:3]
    block_out = (tokens_in.astype(jnp.float32) + gate * projected).astype(jnp.bfloat16)
    forwarded = passed_along(block_out[None, None], "pipe", 1)
    head_rows = lax.dynamic_index_in_dim(head_mod, step_row, 0, keepdims=False)
    normed_out = modulate(block_out, head_rows[0], head_rows[1]).astype(jnp.bfloat16)
    readout = jnp.dot(normed_out, head_weight, preferred_element_type=jnp.float32)
    branch_index = lax.axis_index("cfg")
    half_width = readout.shape[1] // 2
    partner = partner_2(readout.astype(jnp.bfloat16), "cfg", 1).astype(readout.dtype)
    conditional = jnp.where(branch_index == 0, readout, partner)
    unconditional = jnp.where(branch_index == 0, partner, readout)
    combined = unconditional + guidance * (conditional - unconditional)
    guided = lax.dynamic_slice_in_dim(combined, branch_index * half_width, half_width, 1)
    return (forwarded, fresh_pair[None, None], guided[None])


def solution(mesh):
    sizes = (mesh.shape["pipe"], 4, mesh.shape["seq"] // 4, mesh.shape["cfg"])
    grid = Mesh(mesh.devices.reshape(sizes), ("pipe", "y", "x", "cfg"))
    seq = ("y", "x")
    return jax.shard_map(
        per_device,
        mesh=grid,
        in_specs=(
            P("cfg", "pipe", seq, None),
            P("pipe", None, None, seq),
            P("pipe", seq, None),
            P("pipe", None, seq),
            P("cfg", "pipe", None, None, seq),
            P("pipe", None, None, None),
            P(),
            P(),
            P(),
            P(),
        ),
        out_specs=(
            P("cfg", "pipe", seq, None),
            P("cfg", "pipe", None, None, seq),
            P("pipe", seq, "cfg"),
        ),
        check_vma=False,
    )
```
